32 devices in a mesh: blk: 8 (over z, x), sub: 4 (over y, core).
Axes of the slice: x: 2, y: 2, z: 4, core: 2. Of those that a mesh axis runs over, the one named last changes fastest.
Arguments:
- features: bfloat16 [12288, 768], P(('blk', 'sub')), may hold values from -6 to 6
- scales: bfloat16 [12288], P('blk'), may hold values from 0.5 to 4
- neighbor_lists: int32 [9, 16, 12288], P(None, None, 'blk'), may hold values from 0 to 1535, as said below
- eigen_block: float32 [64, 12288], P(None, ('blk', 'sub')), may hold values from -6 to 6
Outputs:
- embedding: float32 [64, 12288], P(None, ('blk', 'sub'))
The draws below stay inside these ranges and needn't reach their ends.
Inputs may be any that keep to these rules, and one draw needn't show every extreme that they name: For each j and point p, the 16 entries neighbor_lists[j, :, p] are distinct positions within the row block that lies j - 4 blocks before p's block, counted cyclically.
All inputs are finite; a program needn't handle non-finite values.
Results may differ from the reference program's by a relative error of at most 0.0039.
Values may be sent and summed in bfloat16 or wider, within the bound.
A program may use at most 128 MiB of HBM per device.

```python
import math
import jax
import jax.numpy as jnp
from jax import lax

F = 768
EIG = 64
HALF = 4
NNB = 16
SHIFTS = 9
BLOCK = 1536
NTOT = 12288
N_BLK = 8


def draw_neighbor_lists(key, part):
    key_start, key_gaps = jax.random.split(jax.random.fold_in(key, 7))
    start = jax.random.randint(key_start, (SHIFTS, 1, NTOT), 0, BLOCK)
    gaps = jax.random.randint(key_gaps, (SHIFTS, NNB, NTOT), 1, BLOCK // NNB)
    offsets = jnp.cumsum(gaps, axis=1) - gaps[:, :1, :]
    return ((start + offsets) % BLOCK).astype(jnp.int32)


def draw_features(key, part):
    key_centre, key_label, key_noise = jax.random.split(jax.random.fold_in(key, 11), 3)
    labels = jax.random.randint(key_label, (NTOT,), 0, EIG)
    centres = jax.random.normal(key_centre, (EIG, F), jnp.float32)
    noise = jax.random.normal(key_noise, (NTOT, F), jnp.float32)
    values = 0.8 * centres[labels] + 0.6 * noise
    return jnp.clip(values, -6.0, 6.0).astype(jnp.bfloat16)


def steps_of(own_key, shape, pieces, least, largest):
    loudness = 1.0
    for axis_at, blocks in pieces:
        heights = jax.random.uniform(jax.random.fold_in(jax.random.fold_in(own_key, 6), axis_at), (blocks,), jnp.float32, least / len(pieces), largest / len(pieces))
        loudness = loudness * jnp.repeat(jnp.exp(heights), shape[axis_at] // blocks).reshape((-1,) + (1,) * (len(shape) - 1 - axis_at))
    return loudness


def normal_values(key, extent, scale, limit, cuts=(), kind=jnp.bfloat16):
    factor_of = steps_of(key, extent, cuts, -0.22, 0.18) if cuts else 1.0
    drawn = jax.random.normal(key, extent, jnp.float32) * scale * factor_of
    return jnp.minimum(jnp.maximum(drawn, -limit), limit).astype(kind)


def setup_inputs(seed: int = 0) -> dict:
    arg_keys = jax.random.split(jax.random.key(seed), 5)
    features = draw_features(jax.random.fold_in(arg_keys[4], 71), 0)
    scales = jnp.clip(jnp.exp(math.log(4.0) - 2.0794415 * jax.random.uniform(arg_keys[1], (NTOT,), jnp.float32) ** steps_of(arg_keys[1], (NTOT,), ((0, 8),), -0.2, 0.2)), 0.5, 4.0).astype(jnp.bfloat16)
    neighbor_lists = draw_neighbor_lists(jax.random.fold_in(arg_keys[4], 71), 0)
    eigen_block = normal_values(arg_keys[3], (EIG, NTOT), 1.0, 6.0, ((1, 32),), jnp.float32)
    return dict(features=features, scales=scales, neighbor_lists=neighbor_lists, eigen_block=eigen_block)


def reference(features, scales, neighbor_lists, eigen_block):
    total = features.shape[0]
    feats = features.astype(jnp.float32)
    norms = lax.optimization_barrier(jnp.sum(feats * feats, axis=1))
    spread = scales.astype(jnp.float32)
    points = jnp.arange(total, dtype=jnp.int32)
    home = (points // BLOCK).astype(jnp.int32)

    def one_list(flat):
        shift_index = flat // NNB
        member = flat % NNB
        offset = shift_index - HALF
        listed = neighbor_lists[shift_index, member].astype(jnp.int32)
        partner = ((home - offset) % N_BLK * BLOCK + listed).astype(jnp.int32)
        inner = lax.optimization_barrier(jnp.sum(feats * feats[partner], axis=1))
        distance = norms + norms[partner] - 2.0 * inner
        return (jnp.exp(-distance / (F * spread * spread[partner])), partner)
    affinity, partners = lax.map(one_list, jnp.arange(SHIFTS * NNB, dtype=jnp.int32))
    row_deg = lax.optimization_barrier(jnp.sum(affinity, axis=0))
    col_deg = jax.ops.segment_sum(affinity.reshape(-1), partners.reshape(-1), num_segments=total)
    degree = 1.0 + 0.5 * (row_deg + col_deg)
    inv_root = lax.rsqrt(degree)
    scaled = eigen_block * inv_root[None, :]
    scaled_low = lax.optimization_barrier(scaled.astype(jnp.bfloat16)).astype(jnp.float32)
    weights_low = lax.optimization_barrier(affinity.astype(jnp.bfloat16)).astype(jnp.float32)

    def accumulate(carry, items):
        row_side, col_side = carry
        weight, partner_row = items
        row_side = row_side + weight[None, :] * scaled_low[:, partner_row]
        spread_terms = jax.ops.segment_sum((weight[None, :] * scaled_low).T, partner_row, num_segments=total)
        return ((row_side, col_side + spread_terms.T), None)
    zeros = jnp.zeros_like(scaled)
    sides, unused = lax.scan(accumulate, (zeros, zeros), (weights_low, partners))
    mixed = inv_root[None, :] * (scaled + 0.5 * (sides[0] + sides[1]))
    gram = jnp.dot(mixed.astype(jnp.float32), mixed.T.astype(jnp.float32), precision=lax.Precision.HIGHEST, preferred_element_type=jnp.float32)
    lower = jnp.linalg.cholesky(gram)
    return math.sqrt(total) * jax.scipy.linalg.solve_triangular(lower, mixed, lower=True)
```

```python
import functools
import math

import jax
import jax.numpy as jnp
from jax import lax
from jax.experimental import pallas as pl
from jax.experimental.pallas import tpu as pltpu
from jax.sharding import PartitionSpec as P

NT = (((1,), (1,)), ((), ()))
LANES = 128
GROUP = 32
CHUNK = 256
MESH = pl.DeviceIdType.MESH


def ring_place(blk, count, folded):
    if not folded:
        return blk
    return jnp.where(blk % 2 == 0, blk // 2, count - 1 - blk // 2)


def ring_block(place, count, folded):
    if not folded:
        return place
    return jnp.where(place < count // 2, 2 * place, 2 * (count - 1 - place) + 1)


def kernel(
    blks, subs, half, feat_dim,
    feats, lists, scale_rows, eigen,
    mixed_out, gram_out,
    block_feats, moving, lists_in, scales_in, own_words, their_words, weight_tiles, half_norms,
    row_deg, deg_send, deg_recv, low_own, block_low, moving_low,
    term_send, term_recv, gram_send_a, gram_a, gram_send_b, gram_b,
    s_feat, r_feat, s_ring, r_ring, s_list, r_list, s_scale, r_scale,
    s_deg, r_deg, s_low, r_low, s_term, r_term, s_gram, r_gram,
):
    rows = feats.shape[0]
    block = rows * subs
    folded = blks == 2 * half
    blk = lax.axis_index("blk")
    sub = lax.axis_index("sub")
    place = ring_place(blk, blks, folded)
    ahead = [ring_block((place + d) % blks, blks, folded) for d in range(half + 1)]
    behind = [ring_block((place + blks - d) % blks, blks, folded) for d in range(half + 1)]
    peers = [(sub + k) % subs for k in range(subs)]
    twice = [(blk - behind[d] + blks) % blks == half for d in range(half + 1)]
    both = [d for d in range(1, half + 1) if not (folded and d == half)]

    barrier = pltpu.get_barrier_semaphore()
    for k in range(1, blks):
        pl.semaphore_signal(barrier, inc=1, device_id={"blk": (blk + k) % blks}, device_id_type=MESH)
    for k in range(1, subs):
        pl.semaphore_signal(barrier, inc=1, device_id={"sub": peers[k]}, device_id_type=MESH)
    pl.semaphore_wait(barrier, blks - 1 + subs - 1)

    def send(src, dst, ssem, rsem, where):
        copy = pltpu.make_async_remote_copy(
            src_ref=src, dst_ref=dst, send_sem=ssem, recv_sem=rsem,
            device_id=where, device_id_type=MESH,
        )
        copy.start()
        return copy

    def span(index):
        return pl.ds(pl.multiple_of(index * rows, rows), rows)

    ring = [send(feats, moving.at[0], s_ring.at[0], r_ring.at[0], {"blk": ahead[1]})]
    gathers = [
        send(feats, block_feats.at[span(sub), :], s_feat.at[k - 1], r_feat.at[k - 1], {"sub": peers[k]})
        for k in range(1, subs)
    ]
    small = []
    for d in range(1, half + 1):
        small.append(send(
            scale_rows.at[:, span(sub)], scales_in.at[d - 1],
            s_scale.at[d - 1], r_scale.at[d - 1], {"blk": ahead[d]},
        ))
    for d in both:
        j = (blk - ahead[d] + blks + half) % blks
        small.append(send(
            lists.at[j, :, span(sub)], lists_in.at[d - 1, 0],
            s_list.at[d - 1, 0], r_list.at[d - 1, 0], {"blk": ahead[d]},
        ))
        if folded:
            small.append(send(
                lists.at[2 * half, :, span(sub)], lists_in.at[d - 1, 1],
                s_list.at[d - 1, 1], r_list.at[d - 1, 1], {"blk": ahead[d]},
            ))
    block_feats[span(sub), :] = feats[...]

    def words_of(j):
        listed = lists[j] - sub * rows
        inside = jnp.logical_and(listed >= 0, listed < rows)
        one = jnp.ones_like(listed)
        bits = jnp.where(inside, jnp.left_shift(one, jnp.right_shift(listed, 4) & 30), 0)
        low = listed & (GROUP - 1)
        spot = lax.broadcasted_iota(jnp.int32, (GROUP, block), 0)
        total = jnp.zeros((GROUP, block), jnp.int32)
        for m in range(listed.shape[0]):
            total = total + jnp.where(low[m : m + 1, :] == spot, bits[m : m + 1, :], 0)
        return total

    for d in range(half + 1):
        own_words[d] = words_of((blk - behind[d] + blks + half) % blks)
        if folded and d > 0:
            @pl.when(twice[d])
            def _():
                own_words[d] = own_words[d] + words_of(2 * half)

    def norm_rows(c, carry):
        at = pl.ds(pl.multiple_of(c * CHUNK, CHUNK), CHUNK)
        part = block_feats[at, :].astype(jnp.float32)
        half_norms[:, at] = lax.dot_general(
            jnp.full((8, part.shape[1]), 0.5, jnp.float32), part * part, NT,
            precision=lax.Precision.HIGHEST, preferred_element_type=jnp.float32,
        )
        return carry

    def tile(d, source):
        values = source[...]
        wide = values.astype(jnp.float32)
        norm_q = 0.5 * jnp.sum(wide * wide, axis=1, keepdims=True)
        scale_q = scale_rows[:, span(sub)] if d == 0 else scales_in[d - 1]
        rate_q = (2.0 / feat_dim) / jnp.transpose(scale_q)[:, :1]
        if d in both:
            def their_of(which):
                listed = jnp.transpose(lists_in[d - 1, which])
                bits = jnp.left_shift(jnp.ones_like(listed), 2 * jnp.right_shift(listed, 7))
                low = listed & (LANES - 1)
                spot = lax.broadcasted_iota(jnp.int32, (rows, LANES), 1)
                words = jnp.zeros((rows, LANES), jnp.int32)
                for m in range(listed.shape[1]):
                    words = words + jnp.where(low[:, m : m + 1] == spot, bits[:, m : m + 1], 0)
                return words

            their_words[...] = their_of(0)
            if folded:
                @pl.when(twice[d])
                def _():
                    their_words[...] = their_words[...] + their_of(1)

        def step(c, col_total):
            at = pl.ds(pl.multiple_of(c * CHUNK, CHUNK), CHUNK)
            inner = lax.dot_general(
                source[...], block_feats[at, :], NT, preferred_element_type=jnp.float32
            )
            rate_p = 1.0 / scale_rows[0:1, at]
            affinity = jnp.exp((inner - half_norms[0:1, at] - norm_q) * (rate_q * rate_p))
            groups = 2 * lax.broadcasted_iota(jnp.int32, (rows // GROUP, GROUP, CHUNK), 0)
            count = jnp.right_shift(own_words[d, :, at][None], groups) & 3
            count = count.reshape(rows, CHUNK)
            if d in both:
                base = c * (CHUNK // LANES)
                their = their_words[...]
                count = count + jnp.concatenate(
                    [jnp.right_shift(their, 2 * (base + i)) & 3 for i in range(CHUNK // LANES)], axis=1
                )
            weight = affinity * count.astype(jnp.float32)
            weight_tiles[d, :, at] = weight.astype(jnp.bfloat16)
            down = jnp.sum(weight, axis=0, keepdims=True)
            row_deg[0:1, at] = down if d == 0 else row_deg[0:1, at] + down
            for i in range(CHUNK // LANES):
                col_total = col_total + weight[:, i * LANES : (i + 1) * LANES]
            return col_total

        col_total = lax.fori_loop(
            0, block // CHUNK, step, jnp.zeros((rows, LANES), jnp.float32)
        )
        return jnp.sum(jnp.transpose(col_total), axis=0, keepdims=True)

    def advance(d):
        ring[d - 1].wait_recv()
        if d < half:
            ring.append(send(
                moving.at[d - 1], moving.at[d], s_ring.at[d], r_ring.at[d], {"blk": ahead[1]}
            ))

    advance(1)
    for copy in gathers:
        copy.wait_recv()
    lax.fori_loop(0, block // CHUNK, norm_rows, 0)
    for copy in small:
        copy.wait_recv()
    own_col = tile(0, feats)

    exchanges = []
    for d in range(1, half + 1):
        if d > 1:
            advance(d)
        col = tile(d, moving.at[d - 1])
        deg_send[d - 1] = jnp.broadcast_to(col, (8, rows))
        exchanges.append(send(
            deg_send.at[d - 1], deg_recv.at[d - 1], s_deg.at[d - 1], r_deg.at[d - 1],
            {"blk": behind[d]},
        ))
    for k in range(1, subs):
        slot = half + k - 1
        deg_send[slot] = jnp.broadcast_to(row_deg[0:1, span(peers[k])], (8, rows))
        exchanges.append(send(
            deg_send.at[slot], deg_recv.at[slot], s_deg.at[slot], r_deg.at[slot],
            {"sub": peers[k]},
        ))
    total = own_col + row_deg[0:1, span(sub)]
    for slot, copy in enumerate(exchanges):
        copy.wait_recv()
        total = total + deg_recv[slot, 0:1, :]
    inv_root = lax.rsqrt(1.0 + 0.5 * total)
    scaled = eigen[...] * inv_root
    low_own[...] = scaled.astype(jnp.bfloat16)

    lows = []
    for d in range(1, half + 1):
        lows.append(send(
            low_own, moving_low.at[d - 1], s_low.at[d - 1], r_low.at[d - 1], {"blk": ahead[d]}
        ))
    for k in range(1, subs):
        slot = half + k - 1
        lows.append(send(
            low_own, block_low.at[sub], s_low.at[slot], r_low.at[slot], {"sub": peers[k]}
        ))
    block_low[sub] = low_own[...]
    for k in range(1, subs):
        lows[half + k - 1].wait_recv()

    def col_term(d):
        acc = None
        for k in range(subs):
            part = lax.dot_general(
                block_low[k], weight_tiles[d, :, k * rows : (k + 1) * rows], NT,
                preferred_element_type=jnp.float32,
            )
            acc = part if acc is None else acc + part
        return acc

    terms = []
    for d in range(1, half + 1):
        term_send[d - 1] = col_term(d)
        terms.append(send(
            term_send.at[d - 1], term_recv.at[d - 1], s_term.at[d - 1], r_term.at[d - 1],
            {"blk": behind[d]},
        ))
    for d in range(1, half + 1):
        lows[d - 1].wait_recv()

    def row_term(index):
        acc = jnp.dot(low_own[...], weight_tiles[0, :, span(index)], preferred_element_type=jnp.float32)
        for d in range(1, half + 1):
            acc = acc + jnp.dot(
                moving_low[d - 1], weight_tiles[d, :, span(index)], preferred_element_type=jnp.float32
            )
        return acc

    for k in range(1, subs):
        slot = half + k - 1
        term_send[slot] = row_term(peers[k])
        terms.append(send(
            term_send.at[slot], term_recv.at[slot], s_term.at[slot], r_term.at[slot],
            {"sub": peers[k]},
        ))
    side = row_term(sub) + col_term(0)
    for slot, copy in enumerate(terms):
        copy.wait_recv()
        side = side + term_recv[slot]
    mixed = inv_root * (scaled + 0.5 * side)
    mixed_out[...] = mixed
    gram = lax.dot_general(
        mixed, mixed, NT, precision=lax.Precision.HIGHEST, preferred_element_type=jnp.float32
    )

    grams = []
    gram_send_a[...] = gram
    for k in range(1, subs):
        grams.append(send(
            gram_send_a, gram_a.at[k - 1], s_gram.at[k - 1], r_gram.at[k - 1], {"sub": peers[k]}
        ))
    for k in range(1, subs):
        grams[k - 1].wait_recv()
        gram = gram + gram_a[k - 1]
    gram_send_b[...] = gram
    for k in range(1, blks):
        slot = subs - 1 + k - 1
        grams.append(send(
            gram_send_b, gram_b.at[k - 1], s_gram.at[slot], r_gram.at[slot],
            {"blk": (blk + k) % blks},
        ))
    for k in range(1, blks):
        grams[subs - 1 + k - 1].wait_recv()
        gram = gram + gram_b[k - 1]
    gram_out[...] = gram
    for copy in ring + gathers + small + exchanges + lows + terms + grams:
        copy.wait_send()


def local(blks, subs, features, scales, neighbor_lists, eigen_block):
    rows, feat_dim = features.shape
    half = (neighbor_lists.shape[0] - 1) // 2
    block = neighbor_lists.shape[2]
    members = neighbor_lists.shape[1]
    eig = eigen_block.shape[0]
    links = half + subs - 1
    scale_rows = jnp.broadcast_to(scales.astype(jnp.float32)[None, :], (8, block))
    dma = pltpu.SemaphoreType.DMA
    here = pl.BlockSpec(memory_space=pltpu.VMEM)
    f32, bf16, i32 = jnp.float32, jnp.bfloat16, jnp.int32
    mixed, gram = pl.pallas_call(
        functools.partial(kernel, blks, subs, half, feat_dim),
        out_shape=(
            jax.ShapeDtypeStruct((eig, rows), f32),
            jax.ShapeDtypeStruct((eig, eig), f32),
        ),
        in_specs=[here] * 4,
        out_specs=(here, here),
        scratch_shapes=[
            pltpu.VMEM((block, feat_dim), bf16),
            pltpu.VMEM((half, rows, feat_dim), bf16),
            pltpu.VMEM((half, 2, members, rows), i32),
            pltpu.VMEM((half, 8, rows), f32),
            pltpu.VMEM((half + 1, GROUP, block), i32),
            pltpu.VMEM((rows, LANES), i32),
            pltpu.VMEM((half + 1, rows, block), bf16),
            pltpu.VMEM((8, block), f32),
            pltpu.VMEM((8, block), f32),
            pltpu.VMEM((links, 8, rows), f32),
            pltpu.VMEM((links, 8, rows), f32),
            pltpu.VMEM((eig, rows), bf16),
            pltpu.VMEM((subs, eig, rows), bf16),
            pltpu.VMEM((half, eig, rows), bf16),
            pltpu.VMEM((links, eig, rows), f32),
            pltpu.VMEM((links, eig, rows), f32),
            pltpu.VMEM((eig, eig), f32),
            pltpu.VMEM((subs - 1, eig, eig), f32),
            pltpu.VMEM((eig, eig), f32),
            pltpu.VMEM((blks - 1, eig, eig), f32),
            dma((subs - 1,)), dma((subs - 1,)),
            dma((half,)), dma((half,)),
            dma((half, 2)), dma((half, 2)),
            dma((half,)), dma((half,)),
            dma((links,)), dma((links,)),
            dma((links,)), dma((links,)),
            dma((links,)), dma((links,)),
            dma((subs + blks - 2,)), dma((subs + blks - 2,)),
        ],
        compiler_params=pltpu.CompilerParams(
            collective_id=0, has_side_effects=True, vmem_limit_bytes=56 * 1024 * 1024
        ),
    )(features, neighbor_lists_of(neighbor_lists), scale_rows, eigen_block)
    lower = jnp.linalg.cholesky(gram)
    total_rows = rows * blks * subs
    return math.sqrt(total_rows) * jax.scipy.linalg.solve_triangular(lower, mixed, lower=True)


def neighbor_lists_of(neighbor_lists):
    return neighbor_lists.astype(jnp.int32)


def solution(mesh):
    placed = (P(("blk", "sub"), None), P("blk"), P(None, None, "blk"), P(None, ("blk", "sub")))
    return jax.shard_map(
        functools.partial(local, mesh.shape["blk"], mesh.shape["sub"]),
        mesh=mesh, in_specs=placed, out_specs=P(None, ("blk", "sub")), check_vma=False,
    )
```

```python
import functools
import math

import jax
import jax.numpy as jnp
from jax import lax
from jax.experimental import pallas as pl
from jax.experimental.pallas import tpu as pltpu
from jax.sharding import PartitionSpec as P

NT = (((1,), (1,)), ((), ()))
LANES = 128
GROUP = 32
CHUNK = 256
MESH = pl.DeviceIdType.MESH


def ring_place(blk, count, folded):
    if not folded:
        return blk
    return jnp.where(blk % 2 == 0, blk // 2, count - 1 - blk // 2)


def ring_block(place, count, folded):
    if not folded:
        return place
    return jnp.where(place < count // 2, 2 * place, 2 * (count - 1 - place) + 1)


def kernel(
    blks, subs, half, feat_dim,
    feats, lists, scale_rows, eigen,
    mixed_out, inverse_out,
    block_feats, moving, lists_in, scales_in, own_words, their_words, weight_tiles, half_norms,
    row_deg, deg_send, deg_recv, low_own, block_low, moving_low,
    term_send, term_recv, gram_send_a, gram_a, gram_send_b, gram_b,
    s_feat, r_feat, s_ring, r_ring, s_list, r_list, s_scale, r_scale,
    s_deg, r_deg, s_low, r_low, s_term, r_term, s_gram, r_gram,
):
    rows = feats.shape[0]
    block = rows * subs
    folded = blks == 2 * half
    blk = lax.axis_index("blk")
    sub = lax.axis_index("sub")
    place = ring_place(blk, blks, folded)
    ahead = [ring_block((place + d) % blks, blks, folded) for d in range(half + 1)]
    behind = [ring_block((place + blks - d) % blks, blks, folded) for d in range(half + 1)]
    peers = [(sub + k) % subs for k in range(subs)]
    twice = [(blk - behind[d] + blks) % blks == half for d in range(half + 1)]
    both = [d for d in range(1, half + 1) if not (folded and d == half)]

    barrier = pltpu.get_barrier_semaphore()
    for k in range(1, blks):
        pl.semaphore_signal(barrier, inc=1, device_id={"blk": (blk + k) % blks}, device_id_type=MESH)
    for k in range(1, subs):
        pl.semaphore_signal(barrier, inc=1, device_id={"sub": peers[k]}, device_id_type=MESH)
    pl.semaphore_wait(barrier, blks - 1 + subs - 1)

    def send(src, dst, ssem, rsem, where):
        copy = pltpu.make_async_remote_copy(
            src_ref=src, dst_ref=dst, send_sem=ssem, recv_sem=rsem,
            device_id=where, device_id_type=MESH,
        )
        copy.start()
        return copy

    def span(index):
        return pl.ds(pl.multiple_of(index * rows, rows), rows)

    ring = [send(feats, moving.at[0], s_ring.at[0], r_ring.at[0], {"blk": ahead[1]})]
    gathers = [
        send(feats, block_feats.at[span(sub), :], s_feat.at[k - 1], r_feat.at[k - 1], {"sub": peers[k]})
        for k in range(1, subs)
    ]
    small = []
    for d in range(1, half + 1):
        small.append(send(
            scale_rows.at[:, span(sub)], scales_in.at[d - 1],
            s_scale.at[d - 1], r_scale.at[d - 1], {"blk": ahead[d]},
        ))
    for d in both:
        j = (blk - ahead[d] + blks + half) % blks
        small.append(send(
            lists.at[j, :, span(sub)], lists_in.at[d - 1, 0],
            s_list.at[d - 1, 0], r_list.at[d - 1, 0], {"blk": ahead[d]},
        ))
        if folded:
            small.append(send(
                lists.at[2 * half, :, span(sub)], lists_in.at[d - 1, 1],
                s_list.at[d - 1, 1], r_list.at[d - 1, 1], {"blk": ahead[d]},
            ))
    block_feats[span(sub), :] = feats[...]

    def words_of(j):
        listed = lists[j] - sub * rows
        inside = jnp.logical_and(listed >= 0, listed < rows)
        one = jnp.ones_like(listed)
        bits = jnp.where(inside, jnp.left_shift(one, jnp.right_shift(listed, 4) & 30), 0)
        low = listed & (GROUP - 1)
        spot = lax.broadcasted_iota(jnp.int32, (GROUP, block), 0)
        total = jnp.zeros((GROUP, block), jnp.int32)
        for m in range(listed.shape[0]):
            total = total + jnp.where(low[m : m + 1, :] == spot, bits[m : m + 1, :], 0)
        return total

    for d in range(half + 1):
        own_words[d] = words_of((blk - behind[d] + blks + half) % blks)
        if folded and d > 0:
            @pl.when(twice[d])
            def _():
                own_words[d] = own_words[d] + words_of(2 * half)

    def norm_rows(c, carry):
        at = pl.ds(pl.multiple_of(c * CHUNK, CHUNK), CHUNK)
        part = block_feats[at, :].astype(jnp.float32)
        half_norms[:, at] = lax.dot_general(
            jnp.full((8, part.shape[1]), 0.5, jnp.float32), part * part, NT,
            precision=lax.Precision.HIGHEST, preferred_element_type=jnp.float32,
        )
        return carry

    def tile(d, source):
        values = source[...]
        wide = values.astype(jnp.float32)
        norm_q = 0.5 * jnp.sum(wide * wide, axis=1, keepdims=True)
        scale_q = scale_rows[:, span(sub)] if d == 0 else scales_in[d - 1]
        rate_q = (2.0 / feat_dim) / jnp.transpose(scale_q)[:, :1]
        if d in both:
            def their_of(which):
                listed = jnp.transpose(lists_in[d - 1, which])
                bits = jnp.left_shift(jnp.ones_like(listed), 2 * jnp.right_shift(listed, 7))
                low = listed & (LANES - 1)
                spot = lax.broadcasted_iota(jnp.int32, (rows, LANES), 1)
                words = jnp.zeros((rows, LANES), jnp.int32)
                for m in range(listed.shape[1]):
                    words = words + jnp.where(low[:, m : m + 1] == spot, bits[:, m : m + 1], 0)
                return words

            their_words[...] = their_of(0)
            if folded:
                @pl.when(twice[d])
                def _():
                    their_words[...] = their_words[...] + their_of(1)

        def step(c, col_total):
            at = pl.ds(pl.multiple_of(c * CHUNK, CHUNK), CHUNK)
            inner = lax.dot_general(
                source[...], block_feats[at, :], NT, preferred_element_type=jnp.float32
            )
            rate_p = 1.0 / scale_rows[0:1, at]
            affinity = jnp.exp((inner - half_norms[0:1, at] - norm_q) * (rate_q * rate_p))
            groups = 2 * lax.broadcasted_iota(jnp.int32, (rows // GROUP, GROUP, CHUNK), 0)
            count = jnp.right_shift(own_words[d, :, at][None], groups) & 3
            count = count.reshape(rows, CHUNK)
            if d in both:
                base = c * (CHUNK // LANES)
                their = their_words[...]
                count = count + jnp.concatenate(
                    [jnp.right_shift(their, 2 * (base + i)) & 3 for i in range(CHUNK // LANES)], axis=1
                )
            weight = affinity * count.astype(jnp.float32)
            weight_tiles[d, :, at] = weight.astype(jnp.bfloat16)
            down = jnp.sum(weight, axis=0, keepdims=True)
            row_deg[0:1, at] = down if d == 0 else row_deg[0:1, at] + down
            for i in range(CHUNK // LANES):
                col_total = col_total + weight[:, i * LANES : (i + 1) * LANES]
            return col_total

        col_total = lax.fori_loop(
            0, block // CHUNK, step, jnp.zeros((rows, LANES), jnp.float32)
        )
        return jnp.sum(jnp.transpose(col_total), axis=0, keepdims=True)

    def advance(d):
        ring[d - 1].wait_recv()
        if d < half:
            ring.append(send(
                moving.at[d - 1], moving.at[d], s_ring.at[d], r_ring.at[d], {"blk": ahead[1]}
            ))

    advance(1)
    for copy in gathers:
        copy.wait_recv()
    lax.fori_loop(0, block // CHUNK, norm_rows, 0)
    for copy in small:
        copy.wait_recv()
    own_col = tile(0, feats)

    exchanges = []
    for d in range(1, half + 1):
        if d > 1:
            advance(d)
        col = tile(d, moving.at[d - 1])
        deg_send[d - 1] = jnp.broadcast_to(col, (8, rows))
        exchanges.append(send(
            deg_send.at[d - 1], deg_recv.at[d - 1], s_deg.at[d - 1], r_deg.at[d - 1],
            {"blk": behind[d]},
        ))
    for k in range(1, subs):
        slot = half + k - 1
        deg_send[slot] = jnp.broadcast_to(row_deg[0:1, span(peers[k])], (8, rows))
        exchanges.append(send(
            deg_send.at[slot], deg_recv.at[slot], s_deg.at[slot], r_deg.at[slot],
            {"sub": peers[k]},
        ))
    total = own_col + row_deg[0:1, span(sub)]
    for slot, copy in enumerate(exchanges):
        copy.wait_recv()
        total = total + deg_recv[slot, 0:1, :]
    inv_root = lax.rsqrt(1.0 + 0.5 * total)
    scaled = eigen[...] * inv_root
    low_own[...] = scaled.astype(jnp.bfloat16)

    lows = []
    for d in range(1, half + 1):
        lows.append(send(
            low_own, moving_low.at[d - 1], s_low.at[d - 1], r_low.at[d - 1], {"blk": ahead[d]}
        ))
    for k in range(1, subs):
        slot = half + k - 1
        lows.append(send(
            low_own, block_low.at[sub], s_low.at[slot], r_low.at[slot], {"sub": peers[k]}
        ))
    block_low[sub] = low_own[...]
    for k in range(1, subs):
        lows[half + k - 1].wait_recv()

    def col_term(d):
        acc = None
        for k in range(subs):
            part = lax.dot_general(
                block_low[k], weight_tiles[d, :, k * rows : (k + 1) * rows], NT,
                preferred_element_type=jnp.float32,
            )
            acc = part if acc is None else acc + part
        return acc

    terms = []
    for d in range(1, half + 1):
        term_send[d - 1] = col_term(d)
        terms.append(send(
            term_send.at[d - 1], term_recv.at[d - 1], s_term.at[d - 1], r_term.at[d - 1],
            {"blk": behind[d]},
        ))
    for d in range(1, half + 1):
        lows[d - 1].wait_recv()

    def row_term(index):
        acc = jnp.dot(low_own[...], weight_tiles[0, :, span(index)], preferred_element_type=jnp.float32)
        for d in range(1, half + 1):
            acc = acc + jnp.dot(
                moving_low[d - 1], weight_tiles[d, :, span(index)], preferred_element_type=jnp.float32
            )
        return acc

    for k in range(1, subs):
        slot = half + k - 1
        term_send[slot] = row_term(peers[k])
        terms.append(send(
            term_send.at[slot], term_recv.at[slot], s_term.at[slot], r_term.at[slot],
            {"sub": peers[k]},
        ))
    side = row_term(sub) + col_term(0)
    for slot, copy in enumerate(terms):
        copy.wait_recv()
        side = side + term_recv[slot]
    mixed = inv_root * (scaled + 0.5 * side)
    mixed_out[...] = mixed
    gram = lax.dot_general(
        mixed, mixed, NT, precision=lax.Precision.HIGHEST, preferred_element_type=jnp.float32
    )

    grams = []
    gram_send_a[...] = gram
    for k in range(1, subs):
        grams.append(send(
            gram_send_a, gram_a.at[k - 1], s_gram.at[k - 1], r_gram.at[k - 1], {"sub": peers[k]}
        ))
    for k in range(1, subs):
        grams[k - 1].wait_recv()
        gram = gram + gram_a[k - 1]
    gram_send_b[...] = gram
    for k in range(1, blks):
        slot = subs - 1 + k - 1
        grams.append(send(
            gram_send_b, gram_b.at[k - 1], s_gram.at[slot], r_gram.at[slot],
            {"blk": (blk + k) % blks},
        ))
    for k in range(1, blks):
        grams[subs - 1 + k - 1].wait_recv()
        gram = gram + gram_b[k - 1]
    eig = gram.shape[0]
    spot_row = lax.broadcasted_iota(jnp.int32, (eig, eig), 0)
    spot_col = lax.broadcasted_iota(jnp.int32, (eig, eig), 1)
    both_parts = jnp.concatenate([gram, (spot_row == spot_col).astype(jnp.float32)], axis=1)
    below = lax.broadcasted_iota(jnp.int32, (eig, 1), 0)
    roots = jnp.zeros((eig, 1), jnp.float32)
    for j in range(eig):
        pivot = both_parts[j : j + 1, j : j + 1]
        roots = jnp.where(below == j, lax.rsqrt(pivot), roots)
        if j + 1 < eig:
            factor = jnp.where(below > j, both_parts[:, j : j + 1], 0.0)
            both_parts = both_parts - factor * (both_parts[j : j + 1, :] * (1.0 / pivot))
    inverse_out[...] = both_parts[:, eig:] * (roots * math.sqrt(rows * subs * blks))
    for copy in ring + gathers + small + exchanges + lows + terms + grams:
        copy.wait_send()


def local(blks, subs, features, scales, neighbor_lists, eigen_block):
    rows, feat_dim = features.shape
    half = (neighbor_lists.shape[0] - 1) // 2
    block = neighbor_lists.shape[2]
    members = neighbor_lists.shape[1]
    eig = eigen_block.shape[0]
    links = half + subs - 1
    scale_rows = jnp.broadcast_to(scales.astype(jnp.float32)[None, :], (8, block))
    dma = pltpu.SemaphoreType.DMA
    here = pl.BlockSpec(memory_space=pltpu.VMEM)
    f32, bf16, i32 = jnp.float32, jnp.bfloat16, jnp.int32
    mixed, inverse = pl.pallas_call(
        functools.partial(kernel, blks, subs, half, feat_dim),
        out_shape=(
            jax.ShapeDtypeStruct((eig, rows), f32),
            jax.ShapeDtypeStruct((eig, eig), f32),
        ),
        in_specs=[here] * 4,
        out_specs=(here, here),
        scratch_shapes=[
            pltpu.VMEM((block, feat_dim), bf16),
            pltpu.VMEM((half, rows, feat_dim), bf16),
            pltpu.VMEM((half, 2, members, rows), i32),
            pltpu.VMEM((half, 8, rows), f32),
            pltpu.VMEM((half + 1, GROUP, block), i32),
            pltpu.VMEM((rows, LANES), i32),
            pltpu.VMEM((half + 1, rows, block), bf16),
            pltpu.VMEM((8, block), f32),
            pltpu.VMEM((8, block), f32),
            pltpu.VMEM((links, 8, rows), f32),
            pltpu.VMEM((links, 8, rows), f32),
            pltpu.VMEM((eig, rows), bf16),
            pltpu.VMEM((subs, eig, rows), bf16),
            pltpu.VMEM((half, eig, rows), bf16),
            pltpu.VMEM((links, eig, rows), f32),
            pltpu.VMEM((links, eig, rows), f32),
            pltpu.VMEM((eig, eig), f32),
            pltpu.VMEM((subs - 1, eig, eig), f32),
            pltpu.VMEM((eig, eig), f32),
            pltpu.VMEM((blks - 1, eig, eig), f32),
            dma((subs - 1,)), dma((subs - 1,)),
            dma((half,)), dma((half,)),
            dma((half, 2)), dma((half, 2)),
            dma((half,)), dma((half,)),
            dma((links,)), dma((links,)),
            dma((links,)), dma((links,)),
            dma((links,)), dma((links,)),
            dma((subs + blks - 2,)), dma((subs + blks - 2,)),
        ],
        compiler_params=pltpu.CompilerParams(
            collective_id=0, has_side_effects=True, vmem_limit_bytes=56 * 1024 * 1024
        ),
    )(features, neighbor_lists_of(neighbor_lists), scale_rows, eigen_block)
    return jnp.dot(
        inverse, mixed, precision=lax.Precision.HIGHEST, preferred_element_type=jnp.float32
    )


def neighbor_lists_of(neighbor_lists):
    return neighbor_lists.astype(jnp.int32)


def solution(mesh):
    placed = (P(("blk", "sub"), None), P("blk"), P(None, None, "blk"), P(None, ("blk", "sub")))
    return jax.shard_map(
        functools.partial(local, mesh.shape["blk"], mesh.shape["sub"]),
        mesh=mesh, in_specs=placed, out_specs=P(None, ("blk", "sub")), check_vma=False,
    )
```

```python
import functools
import math

import jax
import jax.numpy as jnp
from jax import lax
from jax.experimental import pallas as pl
from jax.experimental.pallas import tpu as pltpu
from jax.sharding import PartitionSpec as P

NT = (((1,), (1,)), ((), ()))
LANES = 128
GROUP = 32
CHUNK = 256
MESH = pl.DeviceIdType.MESH


def ring_place(blk, count, folded):
    if not folded:
        return blk
    return jnp.where(blk % 2 == 0, blk // 2, count - 1 - blk // 2)


def ring_block(place, count, folded):
    if not folded:
        return place
    return jnp.where(place < count // 2, 2 * place, 2 * (count - 1 - place) + 1)


def kernel(
    blks, subs, half, feat_dim,
    feats, lists, scale_rows, eigen,
    mixed_out, inverse_out,
    block_feats, moving, back, lists_in, scales_in, own_words, their_words, weight_tiles, half_norms,
    row_deg, deg_send, deg_recv, low_own, block_low, moving_low,
    term_send, term_recv, gram_all, gram_send_a, gram_a, gram_send_b, gram_b, gram_send_c, gram_c,
    s_feat, r_feat, s_ring, r_ring, s_back, r_back, s_list, r_list, s_scale, r_scale,
    s_deg, r_deg, s_low, r_low, s_term, r_term, s_gram, r_gram,
):
    rows = feats.shape[0]
    block = rows * subs
    folded = blks == 2 * half
    blk = lax.axis_index("blk")
    sub = lax.axis_index("sub")
    place = ring_place(blk, blks, folded)
    ahead = [ring_block((place + d) % blks, blks, folded) for d in range(half + 1)]
    behind = [ring_block((place + blks - d) % blks, blks, folded) for d in range(half + 1)]
    peers = [(sub + k) % subs for k in range(subs)]
    twice = [(blk - behind[d] + blks) % blks == half for d in range(half + 1)]
    both = [d for d in range(1, half + 1) if not (folded and d == half)]

    barrier = pltpu.get_barrier_semaphore()
    for k in range(1, blks):
        pl.semaphore_signal(barrier, inc=1, device_id={"blk": (blk + k) % blks}, device_id_type=MESH)
    for k in range(1, subs):
        pl.semaphore_signal(barrier, inc=1, device_id={"sub": peers[k]}, device_id_type=MESH)
    pl.semaphore_wait(barrier, blks - 1 + subs - 1)

    def send(src, dst, ssem, rsem, where):
        copy = pltpu.make_async_remote_copy(
            src_ref=src, dst_ref=dst, send_sem=ssem, recv_sem=rsem,
            device_id=where, device_id_type=MESH,
        )
        copy.start()
        return copy

    def span(index):
        return pl.ds(pl.multiple_of(index * rows, rows), rows)

    near = rows // 4 if folded else rows
    far = pl.ds(near, rows - near)

    def back_send(t):
        last = t == half
        return send(
            feats.at[far, :] if t == 1 else back.at[t - 2],
            moving.at[half - 1, far, :] if last else back.at[t - 1],
            s_back.at[t - 1], r_back.at[t - 1], {"blk": behind[1]},
        )

    backs = [back_send(1)] if folded else []

    def back_advance(t):
        if folded:
            backs[t - 1].wait_recv()
            if t < half:
                backs.append(back_send(t + 1))

    ring = [send(feats, moving.at[0], s_ring.at[0], r_ring.at[0], {"blk": ahead[1]})]
    gathers = [
        send(feats, block_feats.at[span(sub), :], s_feat.at[k - 1], r_feat.at[k - 1], {"sub": peers[k]})
        for k in range(1, subs)
    ]
    small = []
    for d in range(1, half + 1):
        small.append(send(
            scale_rows.at[:, span(sub)], scales_in.at[d - 1],
            s_scale.at[d - 1], r_scale.at[d - 1], {"blk": ahead[d]},
        ))
    for d in both:
        j = (blk - ahead[d] + blks + half) % blks
        small.append(send(
            lists.at[j, :, span(sub)], lists_in.at[d - 1, 0],
            s_list.at[d - 1, 0], r_list.at[d - 1, 0], {"blk": ahead[d]},
        ))
        if folded:
            small.append(send(
                lists.at[2 * half, :, span(sub)], lists_in.at[d - 1, 1],
                s_list.at[d - 1, 1], r_list.at[d - 1, 1], {"blk": ahead[d]},
            ))
    block_feats[span(sub), :] = feats[...]

    def words_of(j):
        listed = lists[j] - sub * rows
        inside = jnp.logical_and(listed >= 0, listed < rows)
        one = jnp.ones_like(listed)
        bits = jnp.where(inside, jnp.left_shift(one, jnp.right_shift(listed, 4) & 30), 0)
        low = listed & (GROUP - 1)
        spot = lax.broadcasted_iota(jnp.int32, (GROUP, block), 0)
        total = jnp.zeros((GROUP, block), jnp.int32)
        for m in range(listed.shape[0]):
            total = total + jnp.where(low[m : m + 1, :] == spot, bits[m : m + 1, :], 0)
        return total

    for d in range(half + 1):
        own_words[d] = words_of((blk - behind[d] + blks + half) % blks)
        if folded and d > 0:
            @pl.when(twice[d])
            def _():
                own_words[d] = own_words[d] + words_of(2 * half)

    def norm_rows(c, carry):
        at = pl.ds(pl.multiple_of(c * CHUNK, CHUNK), CHUNK)
        part = block_feats[at, :].astype(jnp.float32)
        half_norms[:, at] = lax.dot_general(
            jnp.full((8, part.shape[1]), 0.5, jnp.float32), part * part, NT,
            precision=lax.Precision.HIGHEST, preferred_element_type=jnp.float32,
        )
        return carry

    def tile(d, source):
        values = source[...]
        wide = values.astype(jnp.float32)
        norm_q = 0.5 * jnp.sum(wide * wide, axis=1, keepdims=True)
        scale_q = scale_rows[:, span(sub)] if d == 0 else scales_in[d - 1]
        rate_q = (2.0 / feat_dim) / jnp.transpose(scale_q)[:, :1]
        if d in both:
            def their_of(which):
                listed = jnp.transpose(lists_in[d - 1, which])
                bits = jnp.left_shift(jnp.ones_like(listed), 2 * jnp.right_shift(listed, 7))
                low = listed & (LANES - 1)
                spot = lax.broadcasted_iota(jnp.int32, (rows, LANES), 1)
                words = jnp.zeros((rows, LANES), jnp.int32)
                for m in range(listed.shape[1]):
                    words = words + jnp.where(low[:, m : m + 1] == spot, bits[:, m : m + 1], 0)
                return words

            their_words[...] = their_of(0)
            if folded:
                @pl.when(twice[d])
                def _():
                    their_words[...] = their_words[...] + their_of(1)

        def step(c, col_total):
            at = pl.ds(pl.multiple_of(c * CHUNK, CHUNK), CHUNK)
            inner = lax.dot_general(
                source[...], block_feats[at, :], NT, preferred_element_type=jnp.float32
            )
            rate_p = 1.0 / scale_rows[0:1, at]
            affinity = jnp.exp((inner - half_norms[0:1, at] - norm_q) * (rate_q * rate_p))
            groups = 2 * lax.broadcasted_iota(jnp.int32, (rows // GROUP, GROUP, CHUNK), 0)
            count = jnp.right_shift(own_words[d, :, at][None], groups) & 3
            count = count.reshape(rows, CHUNK)
            if d in both:
                base = c * (CHUNK // LANES)
                their = their_words[...]
                count = count + jnp.concatenate(
                    [jnp.right_shift(their, 2 * (base + i)) & 3 for i in range(CHUNK // LANES)], axis=1
                )
            weight = affinity * count.astype(jnp.float32)
            weight_tiles[d, :, at] = weight.astype(jnp.bfloat16)
            down = jnp.sum(weight, axis=0, keepdims=True)
            row_deg[0:1, at] = down if d == 0 else row_deg[0:1, at] + down
            for i in range(CHUNK // LANES):
                col_total = col_total + weight[:, i * LANES : (i + 1) * LANES]
            return col_total

        col_total = lax.fori_loop(
            0, block // CHUNK, step, jnp.zeros((rows, LANES), jnp.float32)
        )
        return jnp.sum(jnp.transpose(col_total), axis=0, keepdims=True)

    def advance(d):
        ring[d - 1].wait_recv()
        if d < half:
            ring.append(send(
                moving.at[d - 1], moving.at[d], s_ring.at[d], r_ring.at[d], {"blk": ahead[1]}
            ) if d < half - 1 else send(
                moving.at[d - 1, pl.ds(0, near), :], moving.at[d, pl.ds(0, near), :],
                s_ring.at[d], r_ring.at[d], {"blk": ahead[1]},
            ))
        back_advance(d)

    advance(1)
    for copy in gathers:
        copy.wait_recv()
    lax.fori_loop(0, block // CHUNK, norm_rows, 0)
    for copy in small:
        copy.wait_recv()
    own_col = tile(0, feats)

    exchanges = []
    for d in range(1, half + 1):
        if d > 1:
            advance(d)
        col = tile(d, moving.at[d - 1])
        deg_send[d - 1] = jnp.broadcast_to(col, (8, rows))
        exchanges.append(send(
            deg_send.at[d - 1], deg_recv.at[d - 1], s_deg.at[d - 1], r_deg.at[d - 1],
            {"blk": behind[d]},
        ))
    for k in range(1, subs):
        slot = half + k - 1
        deg_send[slot] = jnp.broadcast_to(row_deg[0:1, span(peers[k])], (8, rows))
        exchanges.append(send(
            deg_send.at[slot], deg_recv.at[slot], s_deg.at[slot], r_deg.at[slot],
            {"sub": peers[k]},
        ))
    total = own_col + row_deg[0:1, span(sub)]
    for slot, copy in enumerate(exchanges):
        copy.wait_recv()
        total = total + deg_recv[slot, 0:1, :]
    inv_root = lax.rsqrt(1.0 + 0.5 * total)
    scaled = eigen[...] * inv_root
    low_own[...] = scaled.astype(jnp.bfloat16)

    lows = []
    for d in range(1, half + 1):
        lows.append(send(
            low_own, moving_low.at[d - 1], s_low.at[d - 1], r_low.at[d - 1], {"blk": ahead[d]}
        ))
    for k in range(1, subs):
        slot = half + k - 1
        lows.append(send(
            low_own, block_low.at[sub], s_low.at[slot], r_low.at[slot], {"sub": peers[k]}
        ))
    block_low[sub] = low_own[...]
    for k in range(1, subs):
        lows[half + k - 1].wait_recv()

    def col_term(d):
        acc = None
        for k in range(subs):
            part = lax.dot_general(
                block_low[k], weight_tiles[d, :, k * rows : (k + 1) * rows], NT,
                preferred_element_type=jnp.float32,
            )
            acc = part if acc is None else acc + part
        return acc

    terms = []
    for d in range(1, half + 1):
        term_send[d - 1] = col_term(d).astype(jnp.bfloat16)
        terms.append(send(
            term_send.at[d - 1], term_recv.at[d - 1], s_term.at[d - 1], r_term.at[d - 1],
            {"blk": behind[d]},
        ))
    for d in range(1, half + 1):
        lows[d - 1].wait_recv()

    def row_term(index):
        acc = jnp.dot(low_own[...], weight_tiles[0, :, span(index)], preferred_element_type=jnp.float32)
        for d in range(1, half + 1):
            acc = acc + jnp.dot(
                moving_low[d - 1], weight_tiles[d, :, span(index)], preferred_element_type=jnp.float32
            )
        return acc

    for k in range(1, subs):
        slot = half + k - 1
        term_send[slot] = row_term(peers[k]).astype(jnp.bfloat16)
        terms.append(send(
            term_send.at[slot], term_recv.at[slot], s_term.at[slot], r_term.at[slot],
            {"sub": peers[k]},
        ))
    side = row_term(sub) + col_term(0)
    for slot, copy in enumerate(terms):
        copy.wait_recv()
        side = side + term_recv[slot].astype(jnp.float32)
    mixed = inv_root * (scaled + 0.5 * side)
    mixed_out[...] = mixed
    gram = lax.dot_general(
        mixed, mixed, NT, precision=lax.Precision.HIGHEST, preferred_element_type=jnp.float32
    )

    grams = []
    part = gram.shape[0] // subs

    def piece(index):
        return pl.ds(pl.multiple_of(index * part, part), part)

    gram_all[...] = gram
    gram_send_a[...] = gram
    for k in range(1, subs):
        grams.append(send(
            gram_send_a.at[piece(peers[k]), :], gram_a.at[k - 1],
            s_gram.at[k - 1], r_gram.at[k - 1], {"sub": peers[k]},
        ))
    share = gram_all[piece(sub), :]
    for k in range(1, subs):
        grams[k - 1].wait_recv()
        share = share + gram_a[k - 1]
    gram_send_b[...] = share
    for k in range(1, blks):
        slot = subs - 1 + k - 1
        grams.append(send(
            gram_send_b, gram_b.at[k - 1], s_gram.at[slot], r_gram.at[slot],
            {"blk": (blk + k) % blks},
        ))
    for k in range(1, blks):
        grams[subs - 1 + k - 1].wait_recv()
        share = share + gram_b[k - 1]
    gram_send_c[...] = share
    for k in range(1, subs):
        slot = subs - 1 + blks - 1 + k - 1
        grams.append(send(
            gram_send_c, gram_c.at[sub], s_gram.at[slot], r_gram.at[slot], {"sub": peers[k]}
        ))
    gram_c[sub] = share
    for k in range(1, subs):
        grams[subs - 1 + blks - 1 + k - 1].wait_recv()
    gram = gram_c[...].reshape(subs * part, subs * part)
    eig = gram.shape[0]
    spot_row = lax.broadcasted_iota(jnp.int32, (eig, eig), 0)
    spot_col = lax.broadcasted_iota(jnp.int32, (eig, eig), 1)
    both_parts = jnp.concatenate([gram, (spot_row == spot_col).astype(jnp.float32)], axis=1)
    below = lax.broadcasted_iota(jnp.int32, (eig, 1), 0)
    roots = jnp.zeros((eig, 1), jnp.float32)
    for j in range(eig):
        pivot = both_parts[j : j + 1, j : j + 1]
        roots = jnp.where(below == j, lax.rsqrt(pivot), roots)
        if j + 1 < eig:
            factor = jnp.where(below > j, both_parts[:, j : j + 1], 0.0)
            both_parts = both_parts - factor * (both_parts[j : j + 1, :] * (1.0 / pivot))
    inverse_out[...] = both_parts[:, eig:] * (roots * math.sqrt(rows * subs * blks))
    for copy in ring + backs + gathers + small + exchanges + lows + terms + grams:
        copy.wait_send()


def local(blks, subs, features, scales, neighbor_lists, eigen_block):
    rows, feat_dim = features.shape
    half = (neighbor_lists.shape[0] - 1) // 2
    block = neighbor_lists.shape[2]
    members = neighbor_lists.shape[1]
    eig = eigen_block.shape[0]
    links = half + subs - 1
    scale_rows = jnp.broadcast_to(scales.astype(jnp.float32)[None, :], (8, block))
    dma = pltpu.SemaphoreType.DMA
    here = pl.BlockSpec(memory_space=pltpu.VMEM)
    f32, bf16, i32 = jnp.float32, jnp.bfloat16, jnp.int32
    mixed, inverse = pl.pallas_call(
        functools.partial(kernel, blks, subs, half, feat_dim),
        out_shape=(
            jax.ShapeDtypeStruct((eig, rows), f32),
            jax.ShapeDtypeStruct((eig, eig), f32),
        ),
        in_specs=[here] * 4,
        out_specs=(here, here),
        scratch_shapes=[
            pltpu.VMEM((block, feat_dim), bf16),
            pltpu.VMEM((half, rows, feat_dim), bf16),
            pltpu.VMEM((half - 1, rows - rows // 4, feat_dim), bf16),
            pltpu.VMEM((half, 2, members, rows), i32),
            pltpu.VMEM((half, 8, rows), f32),
            pltpu.VMEM((half + 1, GROUP, block), i32),
            pltpu.VMEM((rows, LANES), i32),
            pltpu.VMEM((half + 1, rows, block), bf16),
            pltpu.VMEM((8, block), f32),
            pltpu.VMEM((8, block), f32),
            pltpu.VMEM((links, 8, rows), f32),
            pltpu.VMEM((links, 8, rows), f32),
            pltpu.VMEM((eig, rows), bf16),
            pltpu.VMEM((subs, eig, rows), bf16),
            pltpu.VMEM((half, eig, rows), bf16),
            pltpu.VMEM((links, eig, rows), bf16),
            pltpu.VMEM((links, eig, rows), bf16),
            pltpu.VMEM((eig, eig), f32),
            pltpu.VMEM((eig, eig), f32),
            pltpu.VMEM((subs - 1, eig // subs, eig), f32),
            pltpu.VMEM((eig // subs, eig), f32),
            pltpu.VMEM((blks - 1, eig // subs, eig), f32),
            pltpu.VMEM((eig // subs, eig), f32),
            pltpu.VMEM((subs, eig // subs, eig), f32),
            dma((subs - 1,)), dma((subs - 1,)),
            dma((half,)), dma((half,)),
            dma((half,)), dma((half,)),
            dma((half, 2)), dma((half, 2)),
            dma((half,)), dma((half,)),
            dma((links,)), dma((links,)),
            dma((links,)), dma((links,)),
            dma((links,)), dma((links,)),
            dma((2 * subs + blks - 3,)), dma((2 * subs + blks - 3,)),
        ],
        compiler_params=pltpu.CompilerParams(
            collective_id=0, has_side_effects=True, vmem_limit_bytes=56 * 1024 * 1024
        ),
    )(features, neighbor_lists_of(neighbor_lists), scale_rows, eigen_block)
    return jnp.dot(
        inverse, mixed, precision=lax.Precision.HIGHEST, preferred_element_type=jnp.float32
    )


def neighbor_lists_of(neighbor_lists):
    return neighbor_lists.astype(jnp.int32)


def solution(mesh):
    placed = (P(("blk", "sub"), None), P("blk"), P(None, None, "blk"), P(None, ("blk", "sub")))
    return jax.shard_map(
        functools.partial(local, mesh.shape["blk"], mesh.shape["sub"]),
        mesh=mesh, in_specs=placed, out_specs=P(None, ("blk", "sub")), check_vma=False,
    )
```
